256 devices in a mesh: seq: 32 (over z, x_hi, core), ch: 8 (over x_lo, y).
Axes of the slice: x: 4 (x_hi: 2, x_lo: 2; x = x_hi * 2 + x_lo), y: 4, z: 8, core: 2. Of those that a mesh axis runs over, the one named last changes fastest.
Arguments:
- tokens: bfloat16 [2, 65536, 2048], P(None, 'seq', 'ch'), may hold values from -6 to 6
- inner_forward: bfloat16 [512, 512], replicated, may hold values from -0.25 to 0.25
- outer_forward: bfloat16 [128, 128], replicated, may hold values from -0.5 to 0.5
- twiddle_forward: float32 [128, 512], P('seq'), may hold values from 0.5 to 2
- freq_kernel: bfloat16 [128, 512, 2048], P(None, 'seq', 'ch'), may hold values from -6 to 6
- outer_inverse: bfloat16 [128, 128], replicated, may hold values from -0.5 to 0.5
- inner_inverse: bfloat16 [512, 512], replicated, may hold values from -0.25 to 0.25
- twiddle_inverse: float32 [128, 512], P(None, 'seq'), may hold values from 0.5 to 2
- gate_gain: float32 [2048], P('ch'), may hold values from 0.5 to 1.5
- gate_bias: float32 [2048], P('ch'), may hold values from -1 to 1
- norm_gain: float32 [2048], replicated, may hold values from 0.1 to 1.9
- up_weight: bfloat16 [4, 1024, 512], P(None, 'seq'), may hold values from -0.25 to 0.25
- down_weight: bfloat16 [4, 1024, 512], P(None, 'seq'), may hold values from -0.1875 to 0.1875
Outputs:
- layer_out: bfloat16 [2, 65536, 2048], P(None, 'seq', 'ch')
The draws below stay inside these ranges and needn't reach their ends.
All inputs are finite; a program needn't handle non-finite values.
Results may differ from the reference program's by a relative error of at most 0.008.
Values may be sent and summed in bfloat16 or wider, within the bound.
A program may use at most 128 MiB of HBM per device.

```python
import math
import jax
import jax.numpy as jnp
from jax import lax

NA = 128
NB = 512
D = 2048
H = 4096
BLOCKS = 4
BATCH = 2
SEQ_LEN = 65536


def shard_levels(stream_key, shape, split, smallest, top_value):
    def one(dim, shards_of):
        draws = jax.random.uniform(jax.random.fold_in(jax.random.fold_in(stream_key, 6), dim), (shards_of,), jnp.float32, smallest / len(split), top_value / len(split))
        return jnp.repeat(jnp.exp(draws), shape[dim] // shards_of).reshape((-1,) + (1,) * (len(shape) - dim - 1))

    factor_of = one(*split[0])
    for cut in split[1:]:
        factor_of = factor_of * one(*cut)
    return factor_of


def normal_values(stream_key, dims, spread, most, shards=(), kind=jnp.bfloat16):
    array = spread * jax.random.normal(stream_key, dims, jnp.float32)
    if shards:
        array = array * shard_levels(stream_key, dims, shards, -0.22, 0.18)
    return jnp.clip(array, -most, most).astype(kind)


def setup_inputs(seed: int = 0) -> dict:
    streams_of = jax.random.split(jax.random.key(seed), 14)
    tokens = normal_values(streams_of[0], (BATCH, SEQ_LEN, D), 1.0, 6.0, ((1, 32), (2, 8)))
    inner_forward = normal_values(streams_of[1], (NB, NB), NB ** -0.5, 0.25)
    outer_forward = normal_values(streams_of[2], (NA, NA), NA ** -0.5, 0.5)
    twiddle_forward = jnp.clip(jnp.exp(math.log(2.0) - 1.3862944 * jax.random.uniform(streams_of[3], (NA, NB), jnp.float32) ** shard_levels(streams_of[3], (NA, NB), ((0, 32),), -0.2, 0.2)), 0.5, 2.0)
    freq_kernel = normal_values(streams_of[4], (NA, NB, D), 1.0, 6.0, ((1, 32), (2, 8)))
    outer_inverse = normal_values(streams_of[5], (NA, NA), NA ** -0.5, 0.5)
    inner_inverse = normal_values(streams_of[6], (NB, NB), NB ** -0.5, 0.25)
    twiddle_inverse = jnp.clip(jnp.exp(math.log(2.0) - 1.3862944 * jax.random.uniform(streams_of[7], (NA, NB), jnp.float32) ** shard_levels(streams_of[7], (NA, NB), ((1, 32),), -0.2, 0.2)), 0.5, 2.0)
    gate_gain = jnp.clip(0.5 + 1.0 * jax.random.uniform(streams_of[8], (D,), jnp.float32) ** shard_levels(streams_of[8], (D,), ((0, 8),), -0.2, 0.2), 0.5, 1.5)
    gate_bias = jnp.clip(jax.random.uniform(streams_of[9], (D,), jnp.float32, -1.0, 1.0) * shard_levels(streams_of[9], (D,), ((0, 8),), -0.4, 0.0), -1.0, 1.0)
    norm_gain = jnp.clip(1.0 + 0.18 * jax.random.normal(streams_of[10], (D,), jnp.float32), 0.1, 1.9)
    up_weight = normal_values(streams_of[11], (BLOCKS, H // BLOCKS, D // BLOCKS), (D // BLOCKS) ** -0.5, 0.25, ((1, 32),))
    down_weight = normal_values(streams_of[12], (BLOCKS, H // BLOCKS, D // BLOCKS), (H // BLOCKS) ** -0.5, 0.1875, ((1, 32),))
    return dict(tokens=tokens, inner_forward=inner_forward, outer_forward=outer_forward, twiddle_forward=twiddle_forward, freq_kernel=freq_kernel, outer_inverse=outer_inverse, inner_inverse=inner_inverse, twiddle_inverse=twiddle_inverse, gate_gain=gate_gain, gate_bias=gate_bias, norm_gain=norm_gain, up_weight=up_weight, down_weight=down_weight)


def reference(tokens, inner_forward, outer_forward, twiddle_forward, freq_kernel, outer_inverse, inner_inverse, twiddle_inverse, gate_gain, gate_bias, norm_gain, up_weight, down_weight):
    width_block = D // BLOCKS
    rows_block = min(NA * NB, 4096)

    def one_sequence(sequence):
        grid = sequence.reshape(NA, NB, D).astype(jnp.float32)
        section_one = (jnp.einsum('kb,abc->akc', inner_forward.astype(jnp.float32), grid) * twiddle_forward[:, :, None]).astype(jnp.bfloat16)
        spectrum = (jnp.einsum('ka,abc->kbc', outer_forward.astype(jnp.float32), section_one.astype(jnp.float32)) * freq_kernel.astype(jnp.float32)).astype(jnp.bfloat16)
        section_two = (jnp.einsum('nk,kbc->nbc', outer_inverse.astype(jnp.float32), spectrum.astype(jnp.float32)) * twiddle_inverse[:, :, None]).astype(jnp.bfloat16)
        mixed = jnp.einsum('mk,nkc->nmc', inner_inverse.astype(jnp.float32), section_two.astype(jnp.float32)).reshape(NA * NB, D)
        flat = sequence.astype(jnp.float32)
        gate = jax.nn.sigmoid(flat * gate_gain + gate_bias)
        gated = (flat + gate * mixed).astype(jnp.bfloat16)

        def mlp_block(rows):
            rows_f = rows.astype(jnp.float32)
            scale = lax.rsqrt(lax.optimization_barrier(jnp.mean(rows_f * rows_f, axis=-1, keepdims=True)) + 1e-06)
            normed = (rows_f * scale * norm_gain).astype(jnp.bfloat16)
            normed_b = normed.reshape(-1, BLOCKS, width_block).astype(jnp.float32)
            lifted = jnp.einsum('tbi,bji->tbj', normed_b, up_weight.astype(jnp.float32))
            hidden = jax.nn.gelu(lifted, approximate=True).astype(jnp.bfloat16)
            lowered = jnp.einsum('tbj,bji->tbi', hidden.astype(jnp.float32), down_weight.astype(jnp.float32)).reshape(-1, D)
            return (rows_f + lowered).astype(jnp.bfloat16)
        blocks = gated.reshape(-1, rows_block, D)
        return lax.map(mlp_block, blocks).reshape(NA * NB, D)
    return lax.map(one_sequence, tokens)
```

```python
import functools

import jax
import jax.numpy as jnp
from jax import lax
from jax.experimental import pallas as pl
from jax.experimental.pallas import tpu as pltpu
from jax.sharding import PartitionSpec as P

MESH = pl.DeviceIdType.MESH
BF = jnp.bfloat16
F32 = jnp.float32


def dot(a, b):
    return jnp.dot(a, b, preferred_element_type=F32)


def dot_nt(a, b):
    return lax.dot_general(a, b, (((1,), (1,)), ((), ())), preferred_element_type=F32)


def lanes(col, width):
    return jnp.concatenate([col] * (width // 128), axis=1)


def kernel(
    eps,
    tok, fin, fout, twf, freq, gout, gin, twi, vecs, up, down,
    out,
    x, w_in, w_fo, w_go, w_gi, tw, ti, kraw, vec,
    twb, tib, kt, abuf, bbuf,
    s1, r1, s2, r2, own, other, res, wts, st_own, st_all,
    in_sem, loc_sem, a1_send, a1_recv, a2_send, a2_recv,
    pair_send, pair_recv, st_send, st_recv, wt_send, wt_recv, out_sem,
):
    n_seq, outer_dev = x.shape[0], x.shape[1]
    groups = s1.shape[2]
    kd = s1.shape[3]
    width = x.shape[3]
    inner = x.shape[2]
    outer = fout.shape[0]
    n_ch = st_all.shape[2]
    half = outer_dev // 2

    me = lax.axis_index("seq")
    ch = lax.axis_index("ch")
    z, xh, co = me // 4, (me // 2) % 2, me % 2
    pair = (ch // 2) * 2 + 1 - ch % 2
    block, mine = ch // 2, ch % 2

    loads = [
        pltpu.make_async_copy(tok.at[0], x.at[0], in_sem.at[0]),
        pltpu.make_async_copy(fin, w_in, in_sem.at[1]),
        pltpu.make_async_copy(twf, tw, in_sem.at[2]),
        pltpu.make_async_copy(tok.at[1], x.at[1], in_sem.at[3]),
        pltpu.make_async_copy(fout, w_fo, in_sem.at[4]),
        pltpu.make_async_copy(gout, w_go, in_sem.at[5]),
        pltpu.make_async_copy(gin, w_gi, in_sem.at[6]),
        pltpu.make_async_copy(twi, ti, in_sem.at[7]),
        pltpu.make_async_copy(freq, kraw, in_sem.at[8]),
        pltpu.make_async_copy(vecs, vec, in_sem.at[9]),
        pltpu.make_async_copy(
            up.at[block, :, pl.ds(pl.multiple_of(mine * width, 128), width)],
            wts.at[z, xh, co, 0], in_sem.at[10]),
        pltpu.make_async_copy(
            up.at[block, :, pl.ds(pl.multiple_of((1 - mine) * width, 128), width)],
            wts.at[z, xh, co, 1], in_sem.at[11]),
        pltpu.make_async_copy(
            down.at[block, :, pl.ds(pl.multiple_of(mine * width, 128), width)],
            wts.at[z, xh, co, 2], in_sem.at[12]),
    ]
    for c in loads[10:]:
        c.start()
    for c in loads[:10]:
        c.start()

    bar = pltpu.get_barrier_semaphore()

    def greet_seq(i, _):
        pl.semaphore_signal(bar, inc=1, device_id=((me + i) % groups, ch), device_id_type=MESH)
        return 0

    def greet_ch(i, _):
        pl.semaphore_signal(bar, inc=1, device_id=(me, (ch + i) % n_ch), device_id_type=MESH)
        return 0

    lax.fori_loop(1, groups, greet_seq, 0)
    lax.fori_loop(1, n_ch, greet_ch, 0)

    loads[2].wait()
    for a in range(outer_dev):
        row = jnp.broadcast_to(tw[a : a + 1, :], (128, inner))
        twb[a] = row.T

    pl.semaphore_wait(bar, groups - 1 + n_ch - 1)

    for c in loads[10:]:
        c.wait()

    def weight_to_z(i, _):
        zt = (z + i) % 8
        pltpu.make_async_remote_copy(
            src_ref=wts.at[z, xh, co], dst_ref=wts.at[z, xh, co],
            send_sem=wt_send.at[0], recv_sem=wt_recv.at[0],
            device_id=(zt * 4 + xh * 2 + co, ch), device_id_type=MESH).start()
        return 0

    lax.fori_loop(1, 8, weight_to_z, 0)

    loads[1].wait()
    for s in range(n_seq):
        loads[0 if s == 0 else 3].wait()

        def first(a, _):
            v = dot(w_in[...], x[s, a])
            v = v * lanes(twb[a], width)
            s1[s, a] = v.astype(BF).reshape(groups, kd, width)
            return 0

        lax.fori_loop(0, outer_dev, first, 0)

        def send(i, _):
            j = (me + i) % groups
            pltpu.make_async_remote_copy(
                src_ref=s1.at[s, :, j], dst_ref=r1.at[s, pl.ds(outer_dev * me, outer_dev)],
                send_sem=a1_send.at[s], recv_sem=a1_recv.at[s],
                device_id=(j, ch), device_id_type=MESH).start()
            return 0

        lax.fori_loop(1, groups, send, 0)
        pltpu.make_async_copy(
            s1.at[s, :, me], r1.at[s, pl.ds(outer_dev * me, outer_dev)], loc_sem.at[s]).start()

    side = kd * kd
    ri = lax.broadcasted_iota(jnp.int32, (side, side), 0)
    rj = lax.broadcasted_iota(jnp.int32, (side, side), 1)
    perm = ((ri % kd) * kd + ri // kd == rj).astype(F32).astype(BF)

    def swap(v):
        return dot(perm, v.reshape(side, width)).astype(BF).reshape(kd, kd, width)

    loads[8].wait()

    def prep_kernel(i, _):
        o = pl.multiple_of(i * kd, kd)
        kt[:, pl.ds(o, kd), :] = swap(kraw[pl.ds(o, kd)])
        return 0

    lax.fori_loop(0, outer // kd, prep_kernel, 0)
    loads[7].wait()
    for k in range(kd):
        tib[k] = jnp.broadcast_to(ti[k : k + 1, :], (128, outer)).T

    def line(a, b):
        return wts.at[:, a, b]

    def pull_bytes(count, sem):
        ref = wts.at[pl.ds(0, count), 0, 0]
        pltpu.make_async_copy(ref, ref, sem).wait()

    pull_bytes(7, wt_recv.at[0])
    to_x = pltpu.make_async_remote_copy(
        src_ref=line(xh, co), dst_ref=line(xh, co), send_sem=wt_send.at[1], recv_sem=wt_recv.at[1],
        device_id=(z * 4 + (1 - xh) * 2 + co, ch), device_id_type=MESH)
    to_core = pltpu.make_async_remote_copy(
        src_ref=line(xh, co), dst_ref=line(xh, co), send_sem=wt_send.at[2], recv_sem=wt_recv.at[2],
        device_id=(z * 4 + xh * 2 + 1 - co, ch), device_id_type=MESH)
    relay = pltpu.make_async_remote_copy(
        src_ref=line(1 - xh, co), dst_ref=line(1 - xh, co), send_sem=wt_send.at[3], recv_sem=wt_recv.at[3],
        device_id=(z * 4 + xh * 2 + 1 - co, ch), device_id_type=MESH)
    to_x.start()
    to_core.start()

    loads[4].wait()
    loads[5].wait()

    for s in range(n_seq):
        got = r1.at[s, pl.ds(0, outer - outer_dev)]
        pltpu.make_async_copy(got, got, a1_recv.at[s]).wait()
        pltpu.make_async_copy(
            s1.at[s, :, me], r1.at[s, pl.ds(outer_dev * me, outer_dev)], loc_sem.at[s]).wait()

        def to_k(i, _):
            o = pl.multiple_of(i * kd, kd)
            abuf[:, pl.ds(o, kd), :] = swap(r1[s, pl.ds(o, kd)])
            return 0

        lax.fori_loop(0, outer // kd, to_k, 0)

        def mix(k, _):
            spec = dot(w_fo[...], abuf[k]) * kt[k].astype(F32)
            v = dot(w_go[...], spec.astype(BF)) * lanes(tib[k], width)
            bbuf[k] = v.astype(BF)
            return 0

        lax.fori_loop(0, kd, mix, 0)

        def from_k(i, _):
            o = pl.multiple_of(i * kd, kd)
            s2[s, pl.ds(o, kd)] = swap(bbuf[:, pl.ds(o, kd), :])
            return 0

        lax.fori_loop(0, outer // kd, from_k, 0)

        for h in range(2):
            def send(i, _):
                j = (me + i) % groups
                pltpu.make_async_remote_copy(
                    src_ref=s2.at[s, pl.ds(outer_dev * j + half * h, half)],
                    dst_ref=r2.at[s, pl.ds(half * h, half), me],
                    send_sem=a2_send.at[s, h], recv_sem=a2_recv.at[s, h],
                    device_id=(j, ch), device_id_type=MESH).start()
                return 0

            lax.fori_loop(1, groups, send, 0)
            pltpu.make_async_copy(
                s2.at[s, pl.ds(outer_dev * me + half * h, half)],
                r2.at[s, pl.ds(half * h, half), me], loc_sem.at[n_seq + 2 * s + h]).start()

    to_x.wait_recv()
    relay.start()
    loads[6].wait()
    loads[9].wait()

    def gate(s, h):
        got = r2.at[s, pl.ds(half * h, half), pl.ds(0, groups - 1)]
        pltpu.make_async_copy(got, got, a2_recv.at[s, h]).wait()
        pltpu.make_async_copy(
            s2.at[s, pl.ds(outer_dev * me + half * h, half)],
            r2.at[s, pl.ds(half * h, half), me], loc_sem.at[n_seq + 2 * s + h]).wait()

        def one(n, _):
            mixed = dot(w_gi[...], r2[s, n].reshape(inner, width))
            xf = x[s, n].astype(F32)
            g = jax.nn.sigmoid(xf * vec[0:1, :] + vec[1:2, :])
            y = (xf + g * mixed).astype(BF)
            own[s, n] = y
            pltpu.make_async_remote_copy(
                src_ref=own.at[s, n], dst_ref=other.at[s, n],
                send_sem=pair_send.at[s, n], recv_sem=pair_recv.at[s, n],
                device_id=(me, pair), device_id_type=MESH).start()
            yf = y.astype(F32)
            sq = yf * yf
            part = sq[:, :128]
            for c in range(1, width // 128):
                part = part + sq[:, c * 128 : (c + 1) * 128]
            for b in range(inner // 128):
                t = part[b * 128 : (b + 1) * 128, :].T
                st_own[s, n, :, b * 128 : (b + 1) * 128] = jnp.sum(t, axis=0, keepdims=True)

            def tell(i, _):
                pltpu.make_async_remote_copy(
                    src_ref=st_own.at[s, n], dst_ref=st_all.at[s, n, ch],
                    send_sem=st_send.at[s, n], recv_sem=st_recv.at[s, n],
                    device_id=(me, (ch + i) % n_ch), device_id_type=MESH).start()
                return 0

            lax.fori_loop(1, n_ch, tell, 0)
            st_all[s, n, ch] = st_own[s, n]
            return 0

        lax.fori_loop(half * h, half * (h + 1), one, 0)

    n_q = 4
    zq = 8 // n_q

    def feed(s):
        def one(n, _):
            ref = st_all.at[s, n, pl.ds(0, n_ch - 1)]
            pltpu.make_async_copy(ref, ref, st_recv.at[s, n]).wait()
            total = st_all[s, n, 0]
            for c in range(1, n_ch):
                total = total + st_all[s, n, c]
            scale = lax.rsqrt(total * (1.0 / (n_ch * width)) + eps)
            cols = [
                jnp.broadcast_to(scale[:, b * 128 : (b + 1) * 128], (128, 128)).T
                for b in range(inner // 128)
            ]
            col = lanes(jnp.concatenate(cols, axis=0), width)
            pltpu.make_async_remote_copy(
                src_ref=own.at[s, n], dst_ref=other.at[s, n],
                send_sem=pair_send.at[s, n], recv_sem=pair_recv.at[s, n],
                device_id=(me, pair), device_id_type=MESH).wait()
            yf = own[s, n].astype(F32)
            na = (yf * col * vec[2:3, :]).astype(BF)
            nb = (other[s, n].astype(F32) * col * vec[3:4, :]).astype(BF)
            acc = yf
            for q in range(n_q):
                w = wts[zq * q : zq * (q + 1)]
                rows = zq * 4 * w.shape[4]
                ua = w[:, :, :, 0].reshape(rows, width)
                ub = w[:, :, :, 1].reshape(rows, width)
                dw = w[:, :, :, 2].reshape(rows, width)
                lifted = dot_nt(na, ua) + dot_nt(nb, ub)
                hid = jax.nn.gelu(lifted, approximate=True).astype(BF)
                acc = acc + dot(hid, dw)
            res[s, n] = acc.astype(BF)
            pltpu.make_async_copy(res.at[s, n], out.at[s, n], out_sem).start()
            return 0

        lax.fori_loop(0, outer_dev, one, 0)

    gate(0, 0)
    gate(0, 1)
    to_core.wait_recv()
    relay.wait_recv()
    feed(0)
    gate(1, 0)
    gate(1, 1)
    feed(1)

    pull_bytes(7, wt_send.at[0])
    to_x.wait_send()
    to_core.wait_send()
    relay.wait_send()
    for s in range(n_seq):
        sent = r1.at[s, pl.ds(0, outer - outer_dev)]
        pltpu.make_async_copy(sent, sent, a1_send.at[s]).wait()
        for h in range(2):
            sent = r2.at[s, pl.ds(half * h, half), pl.ds(0, groups - 1)]
            pltpu.make_async_copy(sent, sent, a2_send.at[s, h]).wait()
        for n in range(outer_dev):
            ref = st_all.at[s, n, pl.ds(0, n_ch - 1)]
            pltpu.make_async_copy(ref, ref, st_send.at[s, n]).wait()
    pltpu.make_async_copy(res, out, out_sem).wait()


def local(
    tokens, inner_forward, outer_forward, twiddle_forward, freq_kernel, outer_inverse,
    inner_inverse, twiddle_inverse, gate_gain, gate_bias, norm_gain, up_weight, down_weight,
):
    n_seq, tok_dev, width = tokens.shape
    inner, outer = inner_forward.shape[0], outer_forward.shape[0]
    outer_dev = tok_dev // inner
    groups = outer // outer_dev
    kd = inner // groups
    n_ch = norm_gain.shape[0] // width
    rows = up_weight.shape[1]
    ch = lax.axis_index("ch")
    pair = (ch // 2) * 2 + 1 - ch % 2
    vecs = jnp.stack([
        gate_gain, gate_bias,
        lax.dynamic_slice(norm_gain, (ch * width,), (width,)),
        lax.dynamic_slice(norm_gain, (pair * width,), (width,)),
    ])
    x = tokens.reshape(n_seq, outer_dev, inner, width)
    sems = pltpu.SemaphoreType.DMA
    vm = pltpu.VMEM
    scratch = [
        vm((n_seq, outer_dev, inner, width), BF),
        vm((inner, inner), BF), vm((outer, outer), BF), vm((outer, outer), BF), vm((inner, inner), BF),
        vm((outer_dev, inner), F32), vm((kd, outer), F32), vm((outer, kd, width), BF), vm((4, width), F32),
        vm((outer_dev, inner, 128), F32), vm((kd, outer, 128), F32),
        vm((kd, outer, width), BF), vm((kd, outer, width), BF), vm((kd, outer, width), BF),
        vm((n_seq, outer_dev, groups, kd, width), BF),
        vm((n_seq, outer, kd, width), BF),
        vm((n_seq, outer, kd, width), BF),
        vm((n_seq, outer_dev, groups, kd, width), BF),
        vm((n_seq, outer_dev, inner, width), BF),
        vm((n_seq, outer_dev, inner, width), BF),
        vm((n_seq, outer_dev, inner, width), BF),
        vm((8, 2, 2, 3, rows, width), BF),
        vm((n_seq, outer_dev, 1, inner), F32),
        vm((n_seq, outer_dev, n_ch, 1, inner), F32),
        sems((13,)), sems((3 * n_seq,)),
        sems((n_seq,)), sems((n_seq,)), sems((n_seq, 2)), sems((n_seq, 2)),
        sems((n_seq, outer_dev)), sems((n_seq, outer_dev)),
        sems((n_seq, outer_dev)), sems((n_seq, outer_dev)),
        sems((4,)), sems((4,)), sems,
    ]
    any_spec = pl.BlockSpec(memory_space=pl.ANY)
    y = pl.pallas_call(
        functools.partial(kernel, 1e-06),
        out_shape=jax.ShapeDtypeStruct((n_seq, outer_dev, inner, width), BF),
        in_specs=[any_spec] * 11,
        out_specs=any_spec,
        scratch_shapes=scratch,
        compiler_params=pltpu.CompilerParams(
            collective_id=0, has_side_effects=True, vmem_limit_bytes=60 * 1024 * 1024),
        name="mixer",
    )(
        x, inner_forward, outer_forward, twiddle_forward, freq_kernel, outer_inverse,
        inner_inverse, twiddle_inverse.T, vecs, up_weight, down_weight,
    )
    return y.reshape(n_seq, tok_dev, width)


def solution(mesh):
    in_specs = (
        P(None, "seq", "ch"),
        P(),
        P(),
        P("seq", None),
        P(None, "seq", "ch"),
        P(),
        P(),
        P(None, "seq"),
        P("ch"),
        P("ch"),
        P(),
        P(None, "seq", None),
        P(None, "seq", None),
    )
    out_specs = P(None, "seq", "ch")
    return jax.shard_map(local, mesh=mesh, in_specs=in_specs, out_specs=out_specs, check_vma=False)
```

```python
import functools

import jax
import jax.numpy as jnp
from jax import lax
from jax.experimental import pallas as pl
from jax.experimental.pallas import tpu as pltpu
from jax.sharding import PartitionSpec as P

MESH = pl.DeviceIdType.MESH
BF = jnp.bfloat16
F32 = jnp.float32


def dot(a, b):
    return jnp.dot(a, b, preferred_element_type=F32)


def dot_nt(a, b):
    return lax.dot_general(a, b, (((1,), (1,)), ((), ())), preferred_element_type=F32)


def lanes(col, width):
    return jnp.concatenate([col] * (width // 128), axis=1)


def kernel(
    eps,
    tok, fin, fout, twf, freq, gout, gin, twi, gain, bias, norm, up, down,
    out,
    x, w_in, w_fo, w_go, w_gi, tw, ti, kraw, vec,
    twb, tib, kt, abuf, bbuf,
    s1, r1, s2, r2, own, other, wts, st_own, st_all,
    in_sem, loc_sem, loc2_sem, a1_send, a1_recv, a2_send, a2_recv,
    pair_send, pair_recv, st_send, st_recv, wt_send, wt_recv,
):
    n_seq, outer_dev = x.shape[0], x.shape[1]
    groups = s1.shape[2]
    kd = s1.shape[3]
    width = x.shape[3]
    inner = x.shape[2]
    outer = fout.shape[0]
    n_ch = st_all.shape[2]

    me = lax.axis_index("seq")
    ch = lax.axis_index("ch")
    z, xh, co = me // 4, (me // 2) % 2, me % 2
    pair = (ch // 2) * 2 + 1 - ch % 2
    block, mine = ch // 2, ch % 2

    loads = [
        pltpu.make_async_copy(tok.at[0], x.at[0], in_sem.at[0]),
        pltpu.make_async_copy(fin, w_in, in_sem.at[1]),
        pltpu.make_async_copy(twf, tw, in_sem.at[2]),
        pltpu.make_async_copy(tok.at[1], x.at[1], in_sem.at[3]),
        pltpu.make_async_copy(fout, w_fo, in_sem.at[4]),
        pltpu.make_async_copy(gout, w_go, in_sem.at[5]),
        pltpu.make_async_copy(gin, w_gi, in_sem.at[6]),
        pltpu.make_async_copy(twi, ti, in_sem.at[7]),
        pltpu.make_async_copy(freq, kraw, in_sem.at[8]),
        pltpu.make_async_copy(gain, vec.at[0], in_sem.at[9]),
        pltpu.make_async_copy(bias, vec.at[1], in_sem.at[10]),
        pltpu.make_async_copy(norm.at[ch], vec.at[2], in_sem.at[11]),
        pltpu.make_async_copy(norm.at[pair], vec.at[3], in_sem.at[12]),
    ]
    cols = pl.ds(pl.multiple_of(mine * width, 128), width)
    shard = [
        pltpu.make_async_copy(up.at[block, :, cols], wts.at[z, xh, co, 0], in_sem.at[13]),
        pltpu.make_async_copy(down.at[block, :, cols], wts.at[z, xh, co, 1], in_sem.at[14]),
    ]
    for c in loads[:3] + shard + loads[3:]:
        c.start()

    bar = pltpu.get_barrier_semaphore()

    def greet_seq(i, _):
        pl.semaphore_signal(bar, inc=1, device_id=((me + i) % groups, ch), device_id_type=MESH)
        return 0

    def greet_ch(i, _):
        pl.semaphore_signal(bar, inc=1, device_id=(me, (ch + i) % n_ch), device_id_type=MESH)
        return 0

    lax.fori_loop(1, groups, greet_seq, 0)
    lax.fori_loop(1, n_ch, greet_ch, 0)

    loads[2].wait()
    for a in range(outer_dev):
        row = jnp.broadcast_to(tw[a : a + 1, :], (128, inner))
        twb[a] = row.T

    turn = 1 - 2 * co

    def piece(dz):
        return wts.at[(z + dz + 8) % 8, xh, co, pl.ds(0, 2)]

    def to_z(src, dz, k):
        return pltpu.make_async_remote_copy(
            src_ref=piece(src), dst_ref=piece(src), send_sem=wt_send.at[k], recv_sem=wt_recv.at[k],
            device_id=((z + dz + 8) % 8 * 4 + xh * 2 + co, ch), device_id_type=MESH)

    direct = [to_z(0, turn, 0), to_z(0, -turn, 1), to_z(0, 2 * turn, 2), to_z(0, -2 * turn, 3)]
    passed = [to_z(-2 * turn, turn, 4), to_z(-2 * turn, 2 * turn, 5), to_z(2 * turn, -turn, 6)]

    loads[1].wait()
    for s in range(n_seq):
        loads[0 if s == 0 else 3].wait()

        def first(a, _):
            v = dot(w_in[...], x[s, a])
            v = v * lanes(twb[a], width)
            s1[s, a] = v.astype(BF).reshape(groups, kd, width)
            return 0

        lax.fori_loop(0, outer_dev, first, 0)
        if s == 0:
            pl.semaphore_wait(bar, groups - 1 + n_ch - 1)
            for c in shard:
                c.wait()
            for c in direct:
                c.start()

        def send(i, _):
            j = (me + i) % groups
            pltpu.make_async_remote_copy(
                src_ref=s1.at[s, :, j], dst_ref=r1.at[s, pl.ds(outer_dev * me, outer_dev)],
                send_sem=a1_send.at[s], recv_sem=a1_recv.at[s],
                device_id=(j, ch), device_id_type=MESH).start()
            return 0

        lax.fori_loop(1, groups, send, 0)
        pltpu.make_async_copy(
            s1.at[s, :, me], r1.at[s, pl.ds(outer_dev * me, outer_dev)], loc_sem.at[s]).start()
        if s == 0:
            direct[2].wait_recv()
            passed[0].start()
            passed[1].start()
            direct[3].wait_recv()
            passed[2].start()

    side = kd * kd
    ri = lax.broadcasted_iota(jnp.int32, (side, side), 0)
    rj = lax.broadcasted_iota(jnp.int32, (side, side), 1)
    perm = ((ri % kd) * kd + ri // kd == rj).astype(F32).astype(BF)

    def swap(v):
        return dot(perm, v.reshape(side, width)).astype(BF).reshape(kd, kd, width)

    loads[8].wait()

    def prep_kernel(i, _):
        o = pl.multiple_of(i * kd, kd)
        kt[:, pl.ds(o, kd), :] = swap(kraw[pl.ds(o, kd)])
        return 0

    lax.fori_loop(0, outer // kd, prep_kernel, 0)
    loads[7].wait()
    for k in range(kd):
        tib[k] = jnp.broadcast_to(ti[k : k + 1, :], (128, outer)).T

    def line(a, b):
        return wts.at[:, a, b]

    to_y = pltpu.make_async_remote_copy(
        src_ref=wts.at[:, xh, co, 0], dst_ref=wts.at[:, xh, co, 2],
        send_sem=wt_send.at[7], recv_sem=wt_recv.at[7],
        device_id=(me, pair), device_id_type=MESH)
    to_x = pltpu.make_async_remote_copy(
        src_ref=line(xh, co), dst_ref=line(xh, co), send_sem=wt_send.at[8], recv_sem=wt_recv.at[8],
        device_id=(z * 4 + (1 - xh) * 2 + co, ch), device_id_type=MESH)
    to_core = pltpu.make_async_remote_copy(
        src_ref=line(xh, co), dst_ref=line(xh, co), send_sem=wt_send.at[9], recv_sem=wt_recv.at[9],
        device_id=(z * 4 + xh * 2 + 1 - co, ch), device_id_type=MESH)
    relay = pltpu.make_async_remote_copy(
        src_ref=line(1 - xh, co), dst_ref=line(1 - xh, co), send_sem=wt_send.at[10], recv_sem=wt_recv.at[10],
        device_id=(z * 4 + xh * 2 + 1 - co, ch), device_id_type=MESH)
    for c in direct[:2] + passed:
        c.wait_recv()
    to_y.start()

    loads[4].wait()
    loads[5].wait()

    def keep(s, n):
        return pltpu.make_async_copy(s2.at[s, outer_dev * me + n], r2.at[s, n, me], loc2_sem.at[s, n])

    for s in range(n_seq):
        got = r1.at[s, pl.ds(0, outer - outer_dev)]
        pltpu.make_async_copy(got, got, a1_recv.at[s]).wait()
        pltpu.make_async_copy(
            s1.at[s, :, me], r1.at[s, pl.ds(outer_dev * me, outer_dev)], loc_sem.at[s]).wait()

        def to_k(i, _):
            o = pl.multiple_of(i * kd, kd)
            abuf[:, pl.ds(o, kd), :] = swap(r1[s, pl.ds(o, kd)])
            return 0

        lax.fori_loop(0, outer // kd, to_k, 0)

        def mix(k, _):
            spec = dot(w_fo[...], abuf[k]) * kt[k].astype(F32)
            v = dot(w_go[...], spec.astype(BF)) * lanes(tib[k], width)
            bbuf[k] = v.astype(BF)
            return 0

        lax.fori_loop(0, kd, mix, 0)

        def from_k(i, _):
            o = pl.multiple_of(i * kd, kd)
            s2[s, pl.ds(o, kd)] = swap(bbuf[:, pl.ds(o, kd), :])
            return 0

        lax.fori_loop(0, outer // kd, from_k, 0)

        def send_row(n, _):
            def send(i, _):
                j = (me + i) % groups
                pltpu.make_async_remote_copy(
                    src_ref=s2.at[s, outer_dev * j + n], dst_ref=r2.at[s, n, me],
                    send_sem=a2_send.at[s, n], recv_sem=a2_recv.at[s, n],
                    device_id=(j, ch), device_id_type=MESH).start()
                return 0

            lax.fori_loop(1, groups, send, 0)
            keep(s, n).start()
            return 0

        lax.fori_loop(0, outer_dev, send_row, 0)
        if s == 0:
            to_y.wait_recv()
            to_x.start()
            to_core.start()

    to_x.wait_recv()
    relay.start()
    loads[6].wait()
    for c in loads[9:]:
        c.wait()

    half = inner // 2

    def to_pair(s, n, r):
        rows = pl.ds(r * half, half)
        return pltpu.make_async_remote_copy(
            src_ref=own.at[s, n, rows], dst_ref=other.at[s, n, rows],
            send_sem=pair_send.at[s, n, r], recv_sem=pair_recv.at[s, n, r],
            device_id=(me, pair), device_id_type=MESH)

    def gate(s, n):
        got = r2.at[s, n, pl.ds(0, groups - 1)]
        pltpu.make_async_copy(got, got, a2_recv.at[s, n]).wait()
        keep(s, n).wait()
        sec = r2[s, n].reshape(inner, width)
        for r in range(2):
            rows = slice(r * half, (r + 1) * half)
            mixed = dot(w_gi[rows, :], sec)
            xf = x[s, n, rows].astype(F32)
            g = jax.nn.sigmoid(xf * vec[0] + vec[1])
            y = (xf + g * mixed).astype(BF)
            own[s, n, rows] = y
            yf = y.astype(F32)
            sq = yf * yf
            part = sq[:, :128]
            for c in range(1, width // 128):
                part = part + sq[:, c * 128 : (c + 1) * 128]
            for b in range(half // 128):
                t = part[b * 128 : (b + 1) * 128, :].T
                at = r * half + b * 128
                st_own[s, n, :, at : at + 128] = jnp.sum(t, axis=0, keepdims=True)
            if r == 0:
                to_pair(s, n, 0).start()

        def tell(i, _):
            pltpu.make_async_remote_copy(
                src_ref=st_own.at[s, n], dst_ref=st_all.at[s, n, ch],
                send_sem=st_send.at[s, n], recv_sem=st_recv.at[s, n],
                device_id=(me, (ch + i) % n_ch), device_id_type=MESH).start()
            return 0

        lax.fori_loop(1, n_ch, tell, 0)
        to_pair(s, n, 1).start()
        st_all[s, n, ch] = st_own[s, n]

    n_q = 4
    zq = 8 // n_q

    def feed(s, n):
        ref = st_all.at[s, n, pl.ds(0, n_ch - 1)]
        pltpu.make_async_copy(ref, ref, st_recv.at[s, n]).wait()
        total = st_all[s, n, 0]
        for c in range(1, n_ch):
            total = total + st_all[s, n, c]
        scale = lax.rsqrt(total * (1.0 / (n_ch * width)) + eps)
        for r in range(2):
            rows = slice(r * half, (r + 1) * half)
            cols = [
                jnp.broadcast_to(scale[:, r * half + b * 128 : r * half + (b + 1) * 128], (128, 128)).T
                for b in range(half // 128)
            ]
            col = lanes(jnp.concatenate(cols, axis=0), width)
            to_pair(s, n, r).wait()
            yf = own[s, n, rows].astype(F32)
            na = (yf * col * vec[2]).astype(BF)
            nb = (other[s, n, rows].astype(F32) * col * vec[3]).astype(BF)
            acc = yf
            for q in range(n_q):
                w = wts[zq * q : zq * (q + 1)]
                depth = zq * 4 * w.shape[4]
                ua = w[:, :, :, 0].reshape(depth, width)
                ub = w[:, :, :, 2].reshape(depth, width)
                dw = w[:, :, :, 1].reshape(depth, width)
                lifted = dot_nt(na, ua) + dot_nt(nb, ub)
                hid = jax.nn.gelu(lifted, approximate=True).astype(BF)
                acc = acc + dot(hid, dw)
            out[s, n, rows] = acc.astype(BF)

    gate(0, 0)
    to_core.wait_recv()
    relay.wait_recv()

    def step(t, _):
        gate(t // outer_dev, t % outer_dev)
        feed((t - 1) // outer_dev, (t - 1) % outer_dev)
        return 0

    lax.fori_loop(1, n_seq * outer_dev, step, 0)
    feed(n_seq - 1, outer_dev - 1)

    for c in direct + passed + [to_y, to_x, to_core, relay]:
        c.wait_send()
    for s in range(n_seq):
        sent = r1.at[s, pl.ds(0, outer - outer_dev)]
        pltpu.make_async_copy(sent, sent, a1_send.at[s]).wait()
        for n in range(outer_dev):
            ref = st_all.at[s, n, pl.ds(0, n_ch - 1)]
            pltpu.make_async_copy(ref, ref, st_send.at[s, n]).wait()
            sent = r2.at[s, n, pl.ds(0, groups - 1)]
            pltpu.make_async_copy(sent, sent, a2_send.at[s, n]).wait()


def local(
    tokens, inner_forward, outer_forward, twiddle_forward, freq_kernel, outer_inverse,
    inner_inverse, twiddle_inverse, gate_gain, gate_bias, norm_gain, up_weight, down_weight,
):
    n_seq, tok_dev, width = tokens.shape
    inner, outer = inner_forward.shape[0], outer_forward.shape[0]
    outer_dev = tok_dev // inner
    groups = outer // outer_dev
    kd = inner // groups
    n_ch = norm_gain.shape[0] // width
    rows = up_weight.shape[1]
    x = tokens.reshape(n_seq, outer_dev, inner, width)
    sems = pltpu.SemaphoreType.DMA
    vm = pltpu.VMEM
    scratch = [
        vm((n_seq, outer_dev, inner, width), BF),
        vm((inner, inner), BF), vm((outer, outer), BF), vm((outer, outer), BF), vm((inner, inner), BF),
        vm((outer_dev, inner), F32), vm((kd, outer), F32), vm((outer, kd, width), BF), vm((4, 1, width), F32),
        vm((outer_dev, inner, 128), F32), vm((kd, outer, 128), F32),
        vm((kd, outer, width), BF), vm((kd, outer, width), BF), vm((kd, outer, width), BF),
        vm((n_seq, outer_dev, groups, kd, width), BF),
        vm((n_seq, outer, kd, width), BF),
        vm((n_seq, outer, kd, width), BF),
        vm((n_seq, outer_dev, groups, kd, width), BF),
        vm((n_seq, outer_dev, inner, width), BF),
        vm((n_seq, outer_dev, inner, width), BF),
        vm((8, 2, 2, 3, rows, width), BF),
        vm((n_seq, outer_dev, 1, inner), F32),
        vm((n_seq, outer_dev, n_ch, 1, inner), F32),
        sems((15,)), sems((n_seq,)), sems((n_seq, outer_dev)),
        sems((n_seq,)), sems((n_seq,)), sems((n_seq, outer_dev)), sems((n_seq, outer_dev)),
        sems((n_seq, outer_dev, 2)), sems((n_seq, outer_dev, 2)),
        sems((n_seq, outer_dev)), sems((n_seq, outer_dev)),
        sems((11,)), sems((11,)),
    ]
    y = pl.pallas_call(
        functools.partial(kernel, 1e-06),
        out_shape=jax.ShapeDtypeStruct((n_seq, outer_dev, inner, width), BF),
        in_specs=[pl.BlockSpec(memory_space=pltpu.HBM)] * 13,
        out_specs=pl.BlockSpec(memory_space=pltpu.VMEM),
        scratch_shapes=scratch,
        compiler_params=pltpu.CompilerParams(
            collective_id=0, has_side_effects=True, vmem_limit_bytes=48 * 1024 * 1024),
        name="mixer",
    )(*[pltpu.with_memory_space_constraint(a, pltpu.HBM) for a in (
        x, inner_forward, outer_forward, twiddle_forward, freq_kernel, outer_inverse,
        inner_inverse, twiddle_inverse.T, gate_gain.reshape(1, width), gate_bias.reshape(1, width),
        norm_gain.reshape(n_ch, 1, width), up_weight, down_weight,
    )])
    return y.reshape(n_seq, tok_dev, width)


def solution(mesh):
    in_specs = (
        P(None, "seq", "ch"),
        P(),
        P(),
        P("seq", None),
        P(None, "seq", "ch"),
        P(),
        P(),
        P(None, "seq"),
        P("ch"),
        P("ch"),
        P(),
        P(None, "seq", None),
        P(None, "seq", None),
    )
    out_specs = P(None, "seq", "ch")
    return jax.shard_map(local, mesh=mesh, in_specs=in_specs, out_specs=out_specs, check_vma=False)
```

```python
import functools

import jax
import jax.numpy as jnp
from jax import lax
from jax.experimental import pallas as pl
from jax.experimental.pallas import tpu as pltpu
from jax.sharding import PartitionSpec as P

MESH = pl.DeviceIdType.MESH
BF = jnp.bfloat16
F32 = jnp.float32


def dot(a, b):
    return jnp.dot(a, b, preferred_element_type=F32)


def dot_nt(a, b):
    return lax.dot_general(a, b, (((1,), (1,)), ((), ())), preferred_element_type=F32)


def lanes(col, width):
    return jnp.concatenate([col] * (width // 128), axis=1)


def kernel(
    eps,
    tok, fin, fout, twf, freq, gout, gin, twi, gain, bias, norm, up, down,
    out,
    x, w_in, w_fo, w_go, w_gi, tw, ti, kraw, vec,
    twb, tib, kt, abuf, bbuf,
    s1, r1, s2, r2, own, other, wts, st_own, st_all,
    in_sem, loc_sem, loc2_sem, a1_send, a1_recv, a2_send, a2_recv,
    pair_send, pair_recv, st_send, st_recv, wt_send, wt_recv,
):
    n_seq, outer_dev = x.shape[0], x.shape[1]
    groups = s1.shape[2]
    kd = s1.shape[3]
    width = x.shape[3]
    inner = x.shape[2]
    outer = fout.shape[0]
    n_ch = st_all.shape[2]

    me = lax.axis_index("seq")
    ch = lax.axis_index("ch")
    z, xh, co = me // 4, (me // 2) % 2, me % 2
    pair = (ch // 2) * 2 + 1 - ch % 2
    block, mine = ch // 2, ch % 2

    loads = [
        pltpu.make_async_copy(tok.at[0], x.at[0], in_sem.at[0]),
        pltpu.make_async_copy(fin, w_in, in_sem.at[1]),
        pltpu.make_async_copy(twf, tw, in_sem.at[2]),
        pltpu.make_async_copy(tok.at[1], x.at[1], in_sem.at[3]),
        pltpu.make_async_copy(fout, w_fo, in_sem.at[4]),
        pltpu.make_async_copy(gout, w_go, in_sem.at[5]),
        pltpu.make_async_copy(gin, w_gi, in_sem.at[6]),
        pltpu.make_async_copy(twi, ti, in_sem.at[7]),
        pltpu.make_async_copy(freq, kraw, in_sem.at[8]),
        pltpu.make_async_copy(gain, vec.at[0], in_sem.at[9]),
        pltpu.make_async_copy(bias, vec.at[1], in_sem.at[10]),
        pltpu.make_async_copy(norm.at[ch], vec.at[2], in_sem.at[11]),
        pltpu.make_async_copy(norm.at[pair], vec.at[3], in_sem.at[12]),
    ]
    cols = pl.ds(pl.multiple_of(mine * width, 128), width)
    shard = [
        pltpu.make_async_copy(up.at[block, :, cols], wts.at[z, xh, co, 0], in_sem.at[13]),
        pltpu.make_async_copy(down.at[block, :, cols], wts.at[z, xh, co, 1], in_sem.at[14]),
    ]
    for c in loads[:3]:
        c.start()

    bar = pltpu.get_barrier_semaphore()

    def greet_seq(i, _):
        pl.semaphore_signal(bar, inc=1, device_id=((me + i) % groups, ch), device_id_type=MESH)
        return 0

    def greet_ch(i, _):
        pl.semaphore_signal(bar, inc=1, device_id=(me, (ch + i) % n_ch), device_id_type=MESH)
        return 0

    lax.fori_loop(1, groups, greet_seq, 0)
    lax.fori_loop(1, n_ch, greet_ch, 0)
    for c in shard + loads[3:]:
        c.start()

    turn = 1 - 2 * co

    def piece(dz):
        return wts.at[(z + dz + 8) % 8, xh, co, pl.ds(0, 2)]

    def to_z(src, dz, k):
        return pltpu.make_async_remote_copy(
            src_ref=piece(src), dst_ref=piece(src), send_sem=wt_send.at[k], recv_sem=wt_recv.at[k],
            device_id=((z + dz + 8) % 8 * 4 + xh * 2 + co, ch), device_id_type=MESH)

    direct = [to_z(0, turn, 0), to_z(0, -turn, 1), to_z(0, 2 * turn, 2), to_z(0, -2 * turn, 3)]
    passed = [to_z(-2 * turn, turn, 4), to_z(-2 * turn, 2 * turn, 5), to_z(2 * turn, -turn, 6)]

    early = outer_dev // 2

    def send_one(s, lo, size):
        def send(i, _):
            j = (me + i) % groups
            pltpu.make_async_remote_copy(
                src_ref=s1.at[s, pl.ds(lo, size), j], dst_ref=r1.at[s, pl.ds(outer_dev * me + lo, size)],
                send_sem=a1_send.at[s], recv_sem=a1_recv.at[s],
                device_id=(j, ch), device_id_type=MESH).start()
            return 0

        lax.fori_loop(1, groups, send, 0)

    loads[1].wait()
    for s in range(n_seq):
        loads[0 if s == 0 else 3].wait()

        def first(a, _):
            v = dot(w_in[...], x[s, a])
            v = v * lanes(twb[a], width)
            s1[s, a] = v.astype(BF).reshape(groups, kd, width)
            return 0

        if s == 0:
            loads[2].wait()
            for a in range(outer_dev):
                twb[a] = jnp.broadcast_to(tw[a : a + 1, :], (128, inner)).T
                first(a, 0)
                if a == early - 1:
                    pl.semaphore_wait(bar, groups - 1 + n_ch - 1)
                    for c in shard:
                        c.wait()
                    for c in direct:
                        c.start()
                    send_one(0, 0, early)
            send_one(0, early, outer_dev - early)
        else:
            lax.fori_loop(0, outer_dev, first, 0)
            send_one(s, 0, early)
        pltpu.make_async_copy(
            s1.at[s, :, me], r1.at[s, pl.ds(outer_dev * me, outer_dev)], loc_sem.at[s]).start()
        if s == 0:
            direct[2].wait_recv()
            passed[0].start()
            passed[1].start()
            direct[3].wait_recv()
            passed[2].start()

    side = kd * kd
    ri = lax.broadcasted_iota(jnp.int32, (side, side), 0)
    rj = lax.broadcasted_iota(jnp.int32, (side, side), 1)
    perm = ((ri % kd) * kd + ri // kd == rj).astype(F32).astype(BF)

    def swap(v):
        return dot(perm, v.reshape(side, width)).astype(BF).reshape(kd, kd, width)

    loads[8].wait()

    def prep_kernel(i, _):
        o = pl.multiple_of(i * kd, kd)
        kt[:, pl.ds(o, kd), :] = swap(kraw[pl.ds(o, kd)])
        return 0

    lax.fori_loop(0, outer // kd, prep_kernel, 0)
    loads[7].wait()
    for k in range(kd):
        tib[k] = jnp.broadcast_to(ti[k : k + 1, :], (128, outer)).T

    def line(a, b):
        return wts.at[:, a, b]

    to_y = pltpu.make_async_remote_copy(
        src_ref=wts.at[:, xh, co, 0], dst_ref=wts.at[:, xh, co, 2],
        send_sem=wt_send.at[7], recv_sem=wt_recv.at[7],
        device_id=(me, pair), device_id_type=MESH)
    to_x = pltpu.make_async_remote_copy(
        src_ref=line(xh, co), dst_ref=line(xh, co), send_sem=wt_send.at[8], recv_sem=wt_recv.at[8],
        device_id=(z * 4 + (1 - xh) * 2 + co, ch), device_id_type=MESH)
    to_core = pltpu.make_async_remote_copy(
        src_ref=line(xh, co), dst_ref=line(xh, co), send_sem=wt_send.at[9], recv_sem=wt_recv.at[9],
        device_id=(z * 4 + xh * 2 + 1 - co, ch), device_id_type=MESH)
    relay = pltpu.make_async_remote_copy(
        src_ref=line(1 - xh, co), dst_ref=line(1 - xh, co), send_sem=wt_send.at[10], recv_sem=wt_recv.at[10],
        device_id=(z * 4 + xh * 2 + 1 - co, ch), device_id_type=MESH)
    for c in direct[:2] + passed:
        c.wait_recv()
    to_y.start()

    loads[4].wait()
    loads[5].wait()

    def keep(s, n):
        return pltpu.make_async_copy(s2.at[s, outer_dev * me + n], r2.at[s, n, me], loc2_sem.at[s, n])

    unroll = 8

    def middle(s):
        got = r1.at[s, pl.ds(0, outer - outer_dev)]
        pltpu.make_async_copy(got, got, a1_recv.at[s]).wait()
        pltpu.make_async_copy(
            s1.at[s, :, me], r1.at[s, pl.ds(outer_dev * me, outer_dev)], loc_sem.at[s]).wait()

        for o in range(0, outer, kd):
            abuf[:, o : o + kd, :] = swap(r1[s, o : o + kd])

        def mix(i, _):
            ks = [i * unroll + q for q in range(unroll)]
            spec = [(dot(w_fo[...], abuf[k]) * kt[k].astype(F32)).astype(BF) for k in ks]
            for k, v in zip(ks, spec):
                bbuf[k] = (dot(w_go[...], v) * lanes(tib[k], width)).astype(BF)
            return 0

        lax.fori_loop(0, kd // unroll, mix, 0)

        for o in range(0, outer, kd):
            s2[s, o : o + kd] = swap(bbuf[:, o : o + kd, :])


    def send_two(s, lo, hi):
        def send_row(n, _):
            def send(i, _):
                j = (me + i) % groups
                pltpu.make_async_remote_copy(
                    src_ref=s2.at[s, outer_dev * j + n], dst_ref=r2.at[s, n, me],
                    send_sem=a2_send.at[s, n], recv_sem=a2_recv.at[s, n],
                    device_id=(j, ch), device_id_type=MESH).start()
                return 0

            lax.fori_loop(1, groups, send, 0)
            keep(s, n).start()
            return 0

        lax.fori_loop(lo, hi, send_row, 0)

    half = inner // 2

    def to_pair(s, n, r):
        rows = pl.ds(r * half, half)
        return pltpu.make_async_remote_copy(
            src_ref=own.at[s, n, rows], dst_ref=other.at[s, n, rows],
            send_sem=pair_send.at[s, n, r], recv_sem=pair_recv.at[s, n, r],
            device_id=(me, pair), device_id_type=MESH)

    def gate(s, n):
        got = r2.at[s, n, pl.ds(0, groups - 1)]
        pltpu.make_async_copy(got, got, a2_recv.at[s, n]).wait()
        keep(s, n).wait()
        sec = r2[s, n].reshape(inner, width)
        for r in range(2):
            rows = slice(r * half, (r + 1) * half)
            mixed = dot(w_gi[rows, :], sec)
            xf = x[s, n, rows].astype(F32)
            g = jax.nn.sigmoid(xf * vec[0] + vec[1])
            y = (xf + g * mixed).astype(BF)
            own[s, n, rows] = y
            yf = y.astype(F32)
            sq = yf * yf
            part = sq[:, :128]
            for c in range(1, width // 128):
                part = part + sq[:, c * 128 : (c + 1) * 128]
            for b in range(half // 128):
                t = part[b * 128 : (b + 1) * 128, :].T
                at = r * half + b * 128
                st_own[s, n, :, at : at + 128] = jnp.sum(t, axis=0, keepdims=True)
            if r == 0:
                to_pair(s, n, 0).start()

        def tell(i, _):
            pltpu.make_async_remote_copy(
                src_ref=st_own.at[s, n], dst_ref=st_all.at[s, n, ch],
                send_sem=st_send.at[s, n], recv_sem=st_recv.at[s, n],
                device_id=(me, (ch + i) % n_ch), device_id_type=MESH).start()
            return 0

        lax.fori_loop(1, n_ch, tell, 0)
        to_pair(s, n, 1).start()
        st_all[s, n, ch] = st_own[s, n]

    n_q = 4
    zq = 8 // n_q

    def feed(s, n):
        ref = st_all.at[s, n, pl.ds(0, n_ch - 1)]
        pltpu.make_async_copy(ref, ref, st_recv.at[s, n]).wait()
        total = st_all[s, n, 0]
        for c in range(1, n_ch):
            total = total + st_all[s, n, c]
        scale = lax.rsqrt(total * (1.0 / (n_ch * width)) + eps)
        for r in range(2):
            rows = slice(r * half, (r + 1) * half)
            cols = [
                jnp.broadcast_to(scale[:, r * half + b * 128 : r * half + (b + 1) * 128], (128, 128)).T
                for b in range(half // 128)
            ]
            col = lanes(jnp.concatenate(cols, axis=0), width)
            to_pair(s, n, r).wait()
            yf = own[s, n, rows].astype(F32)
            na = (yf * col * vec[2]).astype(BF)
            nb = (other[s, n, rows].astype(F32) * col * vec[3]).astype(BF)
            acc = yf
            for q in range(n_q):
                w = wts[zq * q : zq * (q + 1)]
                depth = zq * 4 * w.shape[4]
                ua = w[:, :, :, 0].reshape(depth, width)
                ub = w[:, :, :, 2].reshape(depth, width)
                dw = w[:, :, :, 1].reshape(depth, width)
                lifted = dot_nt(na, ua) + dot_nt(nb, ub)
                hid = jax.nn.gelu(lifted, approximate=True).astype(BF)
                acc = acc + dot(hid, dw)
            out[s, n, rows] = acc.astype(BF)

    middle(0)
    to_y.wait_recv()
    to_x.start()
    to_core.start()
    send_two(0, 0, early)
    for s in range(1, n_seq):
        send_one(s, early, outer_dev - early)
    send_two(0, early, outer_dev)
    loads[6].wait()
    for c in loads[9:]:
        c.wait()
    for n in range(early):
        gate(0, n)
    to_x.wait_recv()
    relay.start()
    for s in range(1, n_seq):
        middle(s)
        send_two(s, 0, outer_dev)
    to_core.wait_recv()
    relay.wait_recv()
    for n in range(early - 1):
        feed(0, n)

    def step(t, _):
        gate(t // outer_dev, t % outer_dev)
        feed((t - 1) // outer_dev, (t - 1) % outer_dev)
        return 0

    lax.fori_loop(early, n_seq * outer_dev, step, 0)
    feed(n_seq - 1, outer_dev - 1)

    for c in direct + passed + [to_y, to_x, to_core, relay]:
        c.wait_send()
    for s in range(n_seq):
        sent = r1.at[s, pl.ds(0, outer - outer_dev)]
        pltpu.make_async_copy(sent, sent, a1_send.at[s]).wait()
        for n in range(outer_dev):
            ref = st_all.at[s, n, pl.ds(0, n_ch - 1)]
            pltpu.make_async_copy(ref, ref, st_send.at[s, n]).wait()
            sent = r2.at[s, n, pl.ds(0, groups - 1)]
            pltpu.make_async_copy(sent, sent, a2_send.at[s, n]).wait()


def local(
    tokens, inner_forward, outer_forward, twiddle_forward, freq_kernel, outer_inverse,
    inner_inverse, twiddle_inverse, gate_gain, gate_bias, norm_gain, up_weight, down_weight,
):
    n_seq, tok_dev, width = tokens.shape
    inner, outer = inner_forward.shape[0], outer_forward.shape[0]
    outer_dev = tok_dev // inner
    groups = outer // outer_dev
    kd = inner // groups
    n_ch = norm_gain.shape[0] // width
    rows = up_weight.shape[1]
    x = tokens.reshape(n_seq, outer_dev, inner, width)
    sems = pltpu.SemaphoreType.DMA
    vm = pltpu.VMEM
    scratch = [
        vm((n_seq, outer_dev, inner, width), BF),
        vm((inner, inner), BF), vm((outer, outer), BF), vm((outer, outer), BF), vm((inner, inner), BF),
        vm((outer_dev, inner), F32), vm((kd, outer), F32), vm((outer, kd, width), BF), vm((4, 1, width), F32),
        vm((outer_dev, inner, 128), F32), vm((kd, outer, 128), F32),
        vm((kd, outer, width), BF), vm((kd, outer, width), BF), vm((kd, outer, width), BF),
        vm((n_seq, outer_dev, groups, kd, width), BF),
        vm((n_seq, outer, kd, width), BF),
        vm((n_seq, outer, kd, width), BF),
        vm((n_seq, outer_dev, groups, kd, width), BF),
        vm((n_seq, outer_dev, inner, width), BF),
        vm((n_seq, outer_dev, inner, width), BF),
        vm((8, 2, 2, 3, rows, width), BF),
        vm((n_seq, outer_dev, 1, inner), F32),
        vm((n_seq, outer_dev, n_ch, 1, inner), F32),
        sems((15,)), sems((n_seq,)), sems((n_seq, outer_dev)),
        sems((n_seq,)), sems((n_seq,)), sems((n_seq, outer_dev)), sems((n_seq, outer_dev)),
        sems((n_seq, outer_dev, 2)), sems((n_seq, outer_dev, 2)),
        sems((n_seq, outer_dev)), sems((n_seq, outer_dev)),
        sems((11,)), sems((11,)),
    ]
    y = pl.pallas_call(
        functools.partial(kernel, 1e-06),
        out_shape=jax.ShapeDtypeStruct((n_seq, outer_dev, inner, width), BF),
        in_specs=[pl.BlockSpec(memory_space=pltpu.HBM)] * 13,
        out_specs=pl.BlockSpec(memory_space=pltpu.VMEM),
        scratch_shapes=scratch,
        compiler_params=pltpu.CompilerParams(
            collective_id=0, has_side_effects=True, vmem_limit_bytes=48 * 1024 * 1024),
        name="mixer",
    )(*[pltpu.with_memory_space_constraint(a, pltpu.HBM) for a in (
        x, inner_forward, outer_forward, twiddle_forward, freq_kernel, outer_inverse,
        inner_inverse, twiddle_inverse.T, gate_gain.reshape(1, width), gate_bias.reshape(1, width),
        norm_gain.reshape(n_ch, 1, width), up_weight, down_weight,
    )])
    return y.reshape(n_seq, tok_dev, width)


def solution(mesh):
    in_specs = (
        P(None, "seq", "ch"),
        P(),
        P(),
        P("seq", None),
        P(None, "seq", "ch"),
        P(),
        P(),
        P(None, "seq"),
        P("ch"),
        P("ch"),
        P(),
        P(None, "seq", None),
        P(None, "seq", None),
    )
    out_specs = P(None, "seq", "ch")
    return jax.shard_map(local, mesh=mesh, in_specs=in_specs, out_specs=out_specs, check_vma=False)
```
